32 devices in a mesh: pair: 2 (over x), src: 16 (over z, y, core).
Axes of the slice: x: 2, y: 2, z: 4, core: 2. Of those that a mesh axis runs over, the one named last changes fastest.
Arguments:
- source_feat: bfloat16 [1024, 256], P(('pair', 'src')), parts along dimension 0, may hold values from -6 to 6
- target_feat: bfloat16 [1024, 64, 256], P(('pair', 'src')), parts along dimension 0, may hold values from -6 to 6
- conv_weight: bfloat16 [64, 64], replicated, may hold values from -0.75 to 0.75
- conv_bias: float32 [64], replicated, may hold values from -3 to 3
- proj_weight: bfloat16 [64, 64], replicated, may hold values from -0.75 to 0.75
Outputs:
- cost_tokens: bfloat16 [1024, 32768], P(('pair', 'src')), parts along dimension 0
The draws below stay inside these ranges and needn't reach their ends.
There are 2 independent parts, one for each index of `pair`. The reference program is written for one: setup_inputs(seed, part) draws one part's arguments, and reference() takes and returns one part's arrays. A program takes and returns all parts, laid end to end along the dimension named above; an argument that names none is the same for every part. Nothing has to cross between parts.
All inputs are finite; a program needn't handle non-finite values.
Results may differ from the reference program's by a relative error of at most 0.0051.
Values may be sent and summed in bfloat16 or wider, within the bound.
No kernel may reach another device: no remote copies, remote signals or barrier semaphores. Data moves between devices by JAX's collectives and lax.ppermute only.
A program may use at most 128 MiB of HBM per device.

```python
import jax
import jax.numpy as jnp
from jax import lax

C = 256
EMB = 64
PATCH = 8
S_DEV = 32
S = 512
TP = 512


def block_scale(rng, dims, shards, smallest, top_value):
    loudness = 1.0
    for axis_at, parts in shards:
        draws = jax.random.uniform(jax.random.fold_in(jax.random.fold_in(rng, 6), axis_at), (parts,), jnp.float32, smallest / len(shards), top_value / len(shards))
        loudness = loudness * jnp.repeat(jnp.exp(draws), dims[axis_at] // parts).reshape((-1,) + (1,) * (len(dims) - 1 - axis_at))
    return loudness


def bell_draw(key, extent, deviation, limit, shards=(), held_as=jnp.bfloat16):
    entries = deviation * jax.random.normal(key, extent, jnp.float32)
    if shards:
        entries = entries * block_scale(key, extent, shards, -0.22, 0.18)
    return jnp.clip(entries, -limit, limit).astype(held_as)


def setup_inputs(seed: int = 0, part: int = 0) -> dict:
    splits = jax.random.split(jax.random.key(seed), 6)
    part_keys = jax.random.split(jax.random.fold_in(splits[5], part), 6)
    source_feat = bell_draw(part_keys[0], (S, C), 1.0, 6.0, ((0, 16),))
    target_feat = bell_draw(part_keys[1], (TP, PATCH * PATCH, C), 1.0, 6.0, ((0, 16),))
    conv_weight = bell_draw(splits[2], (PATCH * PATCH, EMB), (PATCH * PATCH) ** -0.5, 0.75)
    conv_bias = bell_draw(splits[3], (EMB,), 0.5, 3.0, (), jnp.float32)
    proj_weight = bell_draw(splits[4], (EMB, EMB), EMB ** -0.5, 0.75)
    return dict(source_feat=source_feat, target_feat=target_feat, conv_weight=conv_weight, conv_bias=conv_bias, proj_weight=proj_weight)


def embed_cost(cost, conv_weight, conv_bias, proj_weight):
    count = cost.shape[0]
    flat = cost.reshape(-1, PATCH * PATCH)
    embedded = jnp.dot(flat, conv_weight, preferred_element_type=jnp.float32) + conv_bias
    hidden = jax.nn.gelu(embedded, approximate=False).astype(jnp.bfloat16)
    result = embedded + jnp.dot(hidden, proj_weight, preferred_element_type=jnp.float32)
    return result.astype(jnp.bfloat16).reshape(count, -1)


def reference(source_feat, target_feat, conv_weight, conv_bias, proj_weight):
    patched = target_feat.reshape(-1, C)
    scale = C ** -0.5

    def encode(block):
        cost = lax.dot_general(block, patched, (((1,), (1,)), ((), ())), preferred_element_type=jnp.float32)
        cost = (cost * scale).astype(jnp.bfloat16)
        return embed_cost(cost, conv_weight, conv_bias, proj_weight)

    blocks = source_feat.reshape(-1, S_DEV, C)
    encoded = lax.map(encode, blocks)
    return encoded.reshape(S, -1)
```

```python
import functools

import jax
import jax.numpy as jnp
from jax import lax
from jax.experimental import pallas as pl
from jax.experimental.pallas import tpu as pltpu
from jax.sharding import PartitionSpec as P

WIDE = 256
COVER = 40
PARAMS = pltpu.CompilerParams(vmem_limit_bytes=20 << 20)
SMALL = pltpu.CompilerParams(vmem_limit_bytes=4 << 20)
SWAP_NUM, SWAP_DEN = 1, 2


def gelu(x):
    return x * (lax.erf(x * 0.7071067811865476) * 0.5 + 0.5)


def block_tokens(source, target, w_ref, b_ref, p_ref, scale):
    cost = lax.dot_general(
        source, target, (((1,), (1,)), ((), ())), preferred_element_type=jnp.float32
    )
    cost = (cost * scale).astype(jnp.bfloat16)
    embedded = jnp.dot(cost, w_ref[...], preferred_element_type=jnp.float32) + b_ref[...]
    hidden = gelu(embedded).astype(jnp.bfloat16)
    out = embedded + jnp.dot(hidden, p_ref[...], preferred_element_type=jnp.float32)
    return out.astype(jnp.bfloat16)


def widen_kernel(w_ref, b_ref, p_ref, ww_ref, wb_ref, wp_ref):
    cells, emb = w_ref.shape
    ww_ref[...] = jnp.zeros_like(ww_ref)
    wp_ref[...] = jnp.zeros_like(wp_ref)
    for i in range(WIDE // cells):
        ww_ref[i * cells:(i + 1) * cells, i * emb:(i + 1) * emb] = w_ref[...]
        wp_ref[i * emb:(i + 1) * emb, i * emb:(i + 1) * emb] = p_ref[...]
        wb_ref[:, i * emb:(i + 1) * emb] = b_ref[...]


def widen(conv_weight, conv_bias, proj_weight):
    return pl.pallas_call(
        widen_kernel,
        out_shape=[
            jax.ShapeDtypeStruct((WIDE, WIDE), conv_weight.dtype),
            jax.ShapeDtypeStruct((1, WIDE), conv_bias.dtype),
            jax.ShapeDtypeStruct((WIDE, WIDE), proj_weight.dtype),
        ],
        compiler_params=SMALL,
    )(conv_weight, conv_bias[None, :], proj_weight)


def far_kernel(src_ref, tgt_ref, w_ref, b_ref, p_ref, out_ref, *, scale):
    out_ref[...] = block_tokens(src_ref[...], tgt_ref[...], w_ref, b_ref, p_ref, scale)


def cost_of(px, cols, chans):
    return pl.CostEstimate(
        flops=COVER * 2 * px * cols * (chans + 2 * WIDE),
        bytes_accessed=2 * px * cols + 2 * cols * chans,
        transcendentals=px * cols,
    )


def direct_tokens(source, patched, first, wide, scale):
    px, chans = source.shape
    cols = patched.shape[0] - first
    skip = first // WIDE
    return pl.pallas_call(
        functools.partial(far_kernel, scale=scale),
        grid=(cols // WIDE,),
        in_specs=[
            pl.BlockSpec((px, chans), lambda i: (0, 0)),
            pl.BlockSpec((WIDE, chans), lambda i: (i + skip, 0)),
            pl.BlockSpec((WIDE, WIDE), lambda i: (0, 0)),
            pl.BlockSpec((1, WIDE), lambda i: (0, 0)),
            pl.BlockSpec((WIDE, WIDE), lambda i: (0, 0)),
        ],
        out_specs=pl.BlockSpec((px, WIDE), lambda i: (0, i)),
        out_shape=jax.ShapeDtypeStruct((px, cols), jnp.bfloat16),
        compiler_params=PARAMS,
        cost_estimate=cost_of(px, cols, chans),
    )(source, patched, *wide)


def near_kernel(src_ref, own_ref, got_ref, w_ref, b_ref, p_ref, *rest, scale, s_dev, own_steps):
    outs, rows_ref = rest[:-1], rest[-1]
    group = len(outs)
    step = pl.program_id(0)

    @pl.when(step == 0)
    def _():
        me = lax.axis_index("src")
        lane = lax.rem(me, group)
        base = me - lane
        for k in range(group):
            to = base + lax.rem(lane + k, group)
            rows_ref[k * s_dev:(k + 1) * s_dev, :] = src_ref[
                pl.ds(pl.multiple_of(to * s_dev, s_dev), s_dev), :
            ]

    target = jnp.where(step < own_steps, own_ref[...], got_ref[...])
    tok = block_tokens(rows_ref[...], target, w_ref, b_ref, p_ref, scale)
    for k in range(group):
        outs[k][...] = tok[k * s_dev:(k + 1) * s_dev, :]


def near_tokens(source, patched, got, s_dev, group, wide, scale):
    px, chans = source.shape
    rows = got.shape[0]
    steps = rows // WIDE
    return pl.pallas_call(
        functools.partial(near_kernel, scale=scale, s_dev=s_dev, own_steps=steps),
        grid=(2 * steps,),
        in_specs=[
            pl.BlockSpec((px, chans), lambda i: (0, 0)),
            pl.BlockSpec((WIDE, chans), lambda i: (jnp.minimum(i, steps - 1), 0)),
            pl.BlockSpec((WIDE, chans), lambda i: (jnp.maximum(i - steps, 0), 0)),
            pl.BlockSpec((WIDE, WIDE), lambda i: (0, 0)),
            pl.BlockSpec((1, WIDE), lambda i: (0, 0)),
            pl.BlockSpec((WIDE, WIDE), lambda i: (0, 0)),
        ],
        out_specs=[pl.BlockSpec((s_dev, WIDE), lambda i: (0, i))] * group,
        out_shape=[jax.ShapeDtypeStruct((s_dev, 2 * rows), jnp.bfloat16)] * group,
        scratch_shapes=[pltpu.VMEM((group * s_dev, chans), source.dtype)],
        compiler_params=PARAMS,
        cost_estimate=cost_of(group * s_dev, 2 * rows, chans),
    )(source, patched, got, *wide)


def place_near_kernel(*refs, cols, stride):
    parts, out_ref, sems = refs[:-2], refs[-2], refs[-1]
    group = len(parts)
    me = lax.axis_index("src")
    lane = lax.rem(me, group)
    base = me - lane
    other = lax.rem(base + group, 2 * group)
    copies = []
    for k, part in enumerate(parts):
        frm = lax.rem(lane + group - k, group)
        for side, start in ((0, base + frm), (1, other + frm)):
            at = pl.multiple_of(start * stride, 128)
            copies.append(pltpu.make_async_copy(
                part.at[:, side * cols:(side + 1) * cols],
                out_ref.at[:, pl.ds(at, cols)],
                sems.at[2 * k + side],
            ))
    for copy in copies:
        copy.start()
    for copy in copies:
        copy.wait()


def place_near(parts, cols, stride, width):
    s_dev = parts[0].shape[0]
    any_spec = pl.BlockSpec(memory_space=pl.ANY)
    return pl.pallas_call(
        functools.partial(place_near_kernel, cols=cols, stride=stride),
        in_specs=[any_spec] * len(parts),
        out_specs=any_spec,
        out_shape=jax.ShapeDtypeStruct((s_dev, width), jnp.bfloat16),
        scratch_shapes=[pltpu.SemaphoreType.DMA((2 * len(parts),))],
        compiler_params=SMALL,
        cost_estimate=pl.CostEstimate(flops=0, bytes_accessed=4 * s_dev * width, transcendentals=0),
    )(*parts)


def place_direct_kernel(part_ref, held_ref, out_ref, sems, *, first, stride):
    n, _, cols = part_ref.shape
    copies = [
        pltpu.make_async_copy(
            part_ref.at[i],
            out_ref.at[:, i * stride + first:i * stride + first + cols],
            sems.at[i],
        )
        for i in range(n)
    ]
    for copy in copies:
        copy.start()
    for copy in copies:
        copy.wait()


def place_direct(part, held, first, stride):
    n, s_dev, cols = part.shape
    any_spec = pl.BlockSpec(memory_space=pl.ANY)
    return pl.pallas_call(
        functools.partial(place_direct_kernel, first=first, stride=stride),
        in_specs=[any_spec] * 2,
        out_specs=any_spec,
        out_shape=jax.ShapeDtypeStruct(held.shape, held.dtype),
        scratch_shapes=[pltpu.SemaphoreType.DMA((n,))],
        input_output_aliases={1: 0},
        compiler_params=SMALL,
        cost_estimate=pl.CostEstimate(flops=0, bytes_accessed=4 * n * s_dev * cols, transcendentals=0),
    )(part, held)


def per_device(source_feat, target_feat, conv_weight, conv_bias, proj_weight):
    patches, cells, chans = target_feat.shape
    emb = conv_weight.shape[1]
    s_dev = source_feat.shape[0]
    scale = chans ** (-0.5)
    n = lax.axis_size("src")
    group = n // 2
    patched = target_feat.reshape(-1, chans)
    swapped = patches * SWAP_NUM // SWAP_DEN * cells
    stride = patches * emb
    first = swapped // cells * emb

    got = lax.ppermute(patched[:swapped], "src", [(i, (i + group) % n) for i in range(n)])
    source = lax.all_to_all(
        jnp.broadcast_to(source_feat[None], (n, s_dev, chans)), "src", 0, 0, tiled=True
    ).reshape(n * s_dev, chans)
    wide = widen(conv_weight, conv_bias, proj_weight)

    direct = direct_tokens(source, patched, swapped, wide, scale).reshape(n, s_dev, -1)
    direct = lax.all_to_all(direct, "src", 0, 0, tiled=True)

    near = near_tokens(source, patched, got, s_dev, group, wide, scale)
    parts = [near[0]]
    for k in range(1, group):
        ring = [(i, i // group * group + (i + k) % group) for i in range(n)]
        parts.append(lax.ppermute(near[k], "src", ring))
    held = place_near(parts, first, stride, n * stride)
    return place_direct(direct, held, first, stride)


def solution(mesh):
    in_specs = (P(("pair", "src"), None), P(("pair", "src"), None, None), P(), P(), P())
    out_specs = P(("pair", "src"), None)
    return jax.shard_map(
        per_device, mesh=mesh, in_specs=in_specs, out_specs=out_specs, check_vma=False
    )
```

```python
import functools

import jax
import jax.numpy as jnp
from jax import lax
from jax.experimental import pallas as pl
from jax.experimental.pallas import tpu as pltpu
from jax.sharding import PartitionSpec as P

WIDE = 256
INNER = 4
SWAP_NUM, SWAP_DEN = 3, 8
COVER = 40
PARAMS = pltpu.CompilerParams(vmem_limit_bytes=20 << 20)
SMALL = pltpu.CompilerParams(vmem_limit_bytes=4 << 20)
ANY = pl.BlockSpec(memory_space=pl.ANY)
HBM = pl.BlockSpec(memory_space=pltpu.HBM)
VMEM = pl.BlockSpec(memory_space=pltpu.VMEM)


def gelu(x):
    return x * (lax.erf(x * 0.7071067811865476) * 0.5 + 0.5)


def block_tokens(source, target, w_ref, b_ref, p_ref, scale):
    cost = lax.dot_general(
        source, target, (((1,), (1,)), ((), ())), preferred_element_type=jnp.float32
    )
    cost = (cost * scale).astype(jnp.bfloat16)
    embedded = jnp.dot(cost, w_ref[...], preferred_element_type=jnp.float32) + b_ref[...]
    hidden = gelu(embedded).astype(jnp.bfloat16)
    out = embedded + jnp.dot(hidden, p_ref[...], preferred_element_type=jnp.float32)
    return out.astype(jnp.bfloat16)


def prepare_kernel(tgt_ref, w_in, b_in, p_in, cross_ref, rest_ref, ww_ref, wb_ref, wp_ref,
                   w_ref, b_ref, p_ref, sems):
    swapped, total = cross_ref.shape[0], tgt_ref.shape[0]
    small = [
        pltpu.make_async_copy(w_in, w_ref, sems.at[0]),
        pltpu.make_async_copy(b_in, b_ref, sems.at[1]),
        pltpu.make_async_copy(p_in, p_ref, sems.at[2]),
    ]
    large = [
        pltpu.make_async_copy(tgt_ref.at[0:swapped, :], cross_ref, sems.at[3]),
        pltpu.make_async_copy(tgt_ref.at[swapped:total, :], rest_ref, sems.at[4]),
    ]
    for copy in small + large:
        copy.start()
    ww_ref[...] = jnp.zeros_like(ww_ref)
    wp_ref[...] = jnp.zeros_like(wp_ref)
    for copy in small:
        copy.wait()
    cells, emb = w_ref.shape
    for i in range(WIDE // cells):
        ww_ref[i * cells:(i + 1) * cells, i * emb:(i + 1) * emb] = w_ref[...]
        wp_ref[i * emb:(i + 1) * emb, i * emb:(i + 1) * emb] = p_ref[...]
        wb_ref[:, i * emb:(i + 1) * emb] = b_ref[...]
    for copy in large:
        copy.wait()


def prepare(patched, swapped, conv_weight, conv_bias, proj_weight):
    rows, chans = patched.shape
    bias = conv_bias[None, :]
    return pl.pallas_call(
        prepare_kernel,
        in_specs=[HBM] * 4,
        out_specs=[VMEM] * 5,
        out_shape=[
            jax.ShapeDtypeStruct((swapped, chans), patched.dtype),
            jax.ShapeDtypeStruct((rows - swapped, chans), patched.dtype),
            jax.ShapeDtypeStruct((WIDE, WIDE), conv_weight.dtype),
            jax.ShapeDtypeStruct((1, WIDE), conv_bias.dtype),
            jax.ShapeDtypeStruct((WIDE, WIDE), proj_weight.dtype),
        ],
        scratch_shapes=[
            pltpu.VMEM(conv_weight.shape, conv_weight.dtype),
            pltpu.VMEM(bias.shape, bias.dtype),
            pltpu.VMEM(proj_weight.shape, proj_weight.dtype),
            pltpu.SemaphoreType.DMA((5,)),
        ],
        compiler_params=SMALL,
    )(*[pltpu.with_memory_space_constraint(x, pltpu.HBM) for x in (patched, conv_weight, bias, proj_weight)])


def cost_of(px, cols, chans):
    return pl.CostEstimate(
        flops=COVER * 2 * px * cols * (chans + 2 * WIDE),
        bytes_accessed=2 * px * cols + 2 * cols * chans,
        transcendentals=px * cols,
    )


def direct_kernel(src_ref, tgt_ref, w_ref, b_ref, p_ref, out_ref, rows_ref, *, scale):
    inner, outer, s_dev, _ = src_ref.shape

    @pl.when(pl.program_id(0) == 0)
    def _():
        mine = lax.axis_index("src") // inner
        for k in range(outer):
            for j in range(inner):
                at = pl.multiple_of(((mine ^ k) * inner + j) * s_dev, s_dev)
                rows_ref[pl.ds(at, s_dev), :] = src_ref[j, k]

    out_ref[...] = block_tokens(rows_ref[...], tgt_ref[...], w_ref, b_ref, p_ref, scale)


def direct_tokens(source, rest, wide, scale):
    inner, outer, s_dev, chans = source.shape
    px = inner * outer * s_dev
    cols = rest.shape[0]
    return pl.pallas_call(
        functools.partial(direct_kernel, scale=scale),
        grid=(cols // WIDE,),
        in_specs=[
            pl.BlockSpec(source.shape, lambda i: (0, 0, 0, 0)),
            pl.BlockSpec((WIDE, chans), lambda i: (i, 0)),
            pl.BlockSpec((WIDE, WIDE), lambda i: (0, 0)),
            pl.BlockSpec((1, WIDE), lambda i: (0, 0)),
            pl.BlockSpec((WIDE, WIDE), lambda i: (0, 0)),
        ],
        out_specs=pl.BlockSpec((px, WIDE), lambda i: (0, i)),
        out_shape=jax.ShapeDtypeStruct((px, cols), jnp.bfloat16),
        scratch_shapes=[pltpu.VMEM((px, chans), source.dtype)],
        compiler_params=PARAMS,
        cost_estimate=cost_of(px, cols, chans),
    )(source, rest, *wide)


def near_kernel(src_ref, tgt_ref, w_ref, b_ref, p_ref, *rest, scale, group):
    outs, rows_ref = rest[-1 - group:-1], rest[-1]
    inner, _, s_dev, _ = src_ref.shape

    @pl.when(pl.program_id(0) == 0)
    def _():
        lane = lax.rem(lax.axis_index("src"), inner)
        for k in range(group):
            rows_ref[k * s_dev:(k + 1) * s_dev, :] = src_ref[lane ^ (k % inner), k // inner]

    tok = block_tokens(rows_ref[...], tgt_ref[...], w_ref, b_ref, p_ref, scale)
    for k in range(group):
        outs[k][...] = tok[k * s_dev:(k + 1) * s_dev, :]


def near_tokens(source, target, held, group, wide, scale):
    _, _, s_dev, chans = source.shape
    rows = target.shape[0]
    steps = rows // WIDE
    skip = steps if held else 0
    return pl.pallas_call(
        functools.partial(near_kernel, scale=scale, group=group),
        grid=(steps,),
        in_specs=[
            pl.BlockSpec(source.shape, lambda i: (0, 0, 0, 0)),
            pl.BlockSpec((WIDE, chans), lambda i: (i, 0)),
            pl.BlockSpec((WIDE, WIDE), lambda i: (0, 0)),
            pl.BlockSpec((1, WIDE), lambda i: (0, 0)),
            pl.BlockSpec((WIDE, WIDE), lambda i: (0, 0)),
        ] + [ANY] * len(held),
        out_specs=[pl.BlockSpec((s_dev, WIDE), lambda i: (0, i + skip))] * group,
        out_shape=[jax.ShapeDtypeStruct((s_dev, 2 * rows), jnp.bfloat16)] * group,
        scratch_shapes=[pltpu.VMEM((group * s_dev, chans), source.dtype)],
        input_output_aliases={5 + k: k for k in range(len(held))},
        compiler_params=PARAMS,
        cost_estimate=cost_of(group * s_dev, rows, chans),
    )(source, target, *wide, *held)


def place_kernel(direct_ref, *refs):
    parts, out_ref, sems = refs[:-2], refs[-2], refs[-1]
    group = len(parts)
    n, _, tail = direct_ref.shape
    first = parts[0].shape[1] // 2
    stride = first + tail
    me = lax.axis_index("src")
    copies = [
        pltpu.make_async_copy(
            direct_ref.at[i], out_ref.at[:, i * stride + first:(i + 1) * stride], sems.at[i]
        )
        for i in range(n)
    ]
    for k, part in enumerate(parts):
        near = me ^ k
        for side, frm in ((0, near), (1, near ^ group)):
            at = pl.multiple_of(frm * stride, 128)
            copies.append(pltpu.make_async_copy(
                part.at[:, side * first:(side + 1) * first],
                out_ref.at[:, pl.ds(at, first)],
                sems.at[n + 2 * k + side],
            ))
    for copy in copies:
        copy.start()
    for copy in copies:
        copy.wait()


def place(direct, parts):
    n, s_dev, tail = direct.shape
    width = n * (tail + parts[0].shape[1] // 2)
    return pl.pallas_call(
        place_kernel,
        in_specs=[ANY] * (1 + len(parts)),
        out_specs=ANY,
        out_shape=jax.ShapeDtypeStruct((s_dev, width), jnp.bfloat16),
        scratch_shapes=[pltpu.SemaphoreType.DMA((n + 2 * len(parts),))],
        compiler_params=SMALL,
        cost_estimate=pl.CostEstimate(flops=0, bytes_accessed=4 * s_dev * width, transcendentals=0),
    )(direct, *parts)


def per_device(source_feat, target_feat, conv_weight, conv_bias, proj_weight):
    patches, cells, chans = target_feat.shape
    s_dev = source_feat.shape[0]
    scale = chans ** (-0.5)
    n = lax.axis_size("src")
    group, outer = n // 2, n // INNER
    swapped = patches * SWAP_NUM // SWAP_DEN * cells

    def exchange(x, bits):
        return lax.ppermute(x, "src", [(i, i ^ bits) for i in range(n)])

    crossed, rest, *wide = prepare(
        target_feat.reshape(-1, chans), swapped, conv_weight, conv_bias, proj_weight
    )
    got = exchange(crossed, group)
    column = jnp.stack([source_feat] + [exchange(source_feat, k * INNER) for k in range(1, outer)])
    rows = [list(range(i, i + INNER)) for i in range(0, n, INNER)]
    source = lax.all_gather(column, "src", axis=0, axis_index_groups=rows)

    direct = direct_tokens(source, rest, wide, scale).reshape(n, s_dev, -1)
    direct = lax.all_to_all(direct, "src", 0, 0, tiled=True)

    near = near_tokens(source, crossed, [], group, wide, scale)
    near = near_tokens(source, got, near, group, wide, scale)
    parts = [near[0]] + [exchange(near[k], k) for k in range(1, group)]
    return place(direct, parts)


def solution(mesh):
    in_specs = (P(("pair", "src"), None), P(("pair", "src"), None, None), P(), P(), P())
    out_specs = P(("pair", "src"), None)
    return jax.shard_map(
        per_device, mesh=mesh, in_specs=in_specs, out_specs=out_specs, check_vma=False
    )
```

```python
import functools

import jax
import jax.numpy as jnp
from jax import lax
from jax.experimental import pallas as pl
from jax.experimental.pallas import tpu as pltpu
from jax.sharding import PartitionSpec as P

WIDE = 256
INNER = 4
SWAP_NUM, SWAP_DEN = 3, 8
COVER = 40
PARAMS = pltpu.CompilerParams(vmem_limit_bytes=20 << 20)
SMALL = pltpu.CompilerParams(vmem_limit_bytes=4 << 20)
ANY = pl.BlockSpec(memory_space=pl.ANY)
HBM = pl.BlockSpec(memory_space=pltpu.HBM)
VMEM = pl.BlockSpec(memory_space=pltpu.VMEM)


def partners(group):
    return list(range(group))[::-1]


def gelu(x):
    return x * (lax.erf(x * 0.7071067811865476) * 0.5 + 0.5)


def pipeline_tokens(source, target_ref, w_ref, b_ref, p_ref, scale, store):
    blocks = target_ref.shape[0] // WIDE
    cost, embedded, hidden = {}, {}, {}
    for i in range(blocks + 2):
        if i < blocks:
            product = lax.dot_general(
                source, target_ref[i * WIDE:(i + 1) * WIDE, :], (((1,), (1,)), ((), ())),
                preferred_element_type=jnp.float32,
            )
            cost[i] = (product * scale).astype(jnp.bfloat16)
        if 0 <= i - 1 < blocks:
            embed = jnp.dot(cost.pop(i - 1), w_ref[...], preferred_element_type=jnp.float32)
            embedded[i - 1] = embed + b_ref[...]
            hidden[i - 1] = gelu(embedded[i - 1]).astype(jnp.bfloat16)
        if 0 <= i - 2:
            mixed = jnp.dot(hidden.pop(i - 2), p_ref[...], preferred_element_type=jnp.float32)
            store(i - 2, (embedded.pop(i - 2) + mixed).astype(jnp.bfloat16))


def prepare_kernel(tgt_ref, w_in, b_in, p_in, cross_ref, rest_ref, ww_ref, wb_ref, wp_ref,
                   w_ref, b_ref, p_ref, sems):
    swapped, total = cross_ref.shape[0], tgt_ref.shape[0]
    small = [
        pltpu.make_async_copy(w_in, w_ref, sems.at[0]),
        pltpu.make_async_copy(b_in, b_ref, sems.at[1]),
        pltpu.make_async_copy(p_in, p_ref, sems.at[2]),
    ]
    large = [
        pltpu.make_async_copy(tgt_ref.at[0:swapped, :], cross_ref, sems.at[3]),
        pltpu.make_async_copy(tgt_ref.at[swapped:total, :], rest_ref, sems.at[4]),
    ]
    for copy in small + large:
        copy.start()
    ww_ref[...] = jnp.zeros_like(ww_ref)
    wp_ref[...] = jnp.zeros_like(wp_ref)
    for copy in small:
        copy.wait()
    cells, emb = w_ref.shape
    for i in range(WIDE // cells):
        ww_ref[i * cells:(i + 1) * cells, i * emb:(i + 1) * emb] = w_ref[...]
        wp_ref[i * emb:(i + 1) * emb, i * emb:(i + 1) * emb] = p_ref[...]
        wb_ref[:, i * emb:(i + 1) * emb] = b_ref[...]
    for copy in large:
        copy.wait()


def prepare(patched, swapped, conv_weight, conv_bias, proj_weight):
    rows, chans = patched.shape
    bias = conv_bias[None, :]
    return pl.pallas_call(
        prepare_kernel,
        in_specs=[HBM] * 4,
        out_specs=[VMEM] * 5,
        out_shape=[
            jax.ShapeDtypeStruct((swapped, chans), patched.dtype),
            jax.ShapeDtypeStruct((rows - swapped, chans), patched.dtype),
            jax.ShapeDtypeStruct((WIDE, WIDE), conv_weight.dtype),
            jax.ShapeDtypeStruct((1, WIDE), conv_bias.dtype),
            jax.ShapeDtypeStruct((WIDE, WIDE), proj_weight.dtype),
        ],
        scratch_shapes=[
            pltpu.VMEM(conv_weight.shape, conv_weight.dtype),
            pltpu.VMEM(bias.shape, bias.dtype),
            pltpu.VMEM(proj_weight.shape, proj_weight.dtype),
            pltpu.SemaphoreType.DMA((5,)),
        ],
        compiler_params=SMALL,
    )(*[pltpu.with_memory_space_constraint(x, pltpu.HBM) for x in (patched, conv_weight, bias, proj_weight)])


def cost_of(px, cols, chans):
    return pl.CostEstimate(
        flops=COVER * 2 * px * cols * (chans + 2 * WIDE),
        bytes_accessed=2 * px * cols + 2 * cols * chans,
        transcendentals=px * cols,
    )


def direct_kernel(src_ref, tgt_ref, w_ref, b_ref, p_ref, out_ref, *, scale):
    inner, outer, s_dev, chans = src_ref.shape
    height = out_ref.shape[0] // s_dev
    mine = lax.axis_index("src") // inner
    begin = pl.program_id(0) * height
    rows = []
    for r in range(height):
        place = begin + r
        rows.append(src_ref[lax.rem(place, inner), mine ^ (place // inner)])

    def store(i, tok):
        out_ref[:, i * WIDE:(i + 1) * WIDE] = tok

    pipeline_tokens(jnp.concatenate(rows), tgt_ref, w_ref, b_ref, p_ref, scale, store)


def direct_tokens(source, rest, wide, scale):
    inner, outer, s_dev, chans = source.shape
    px = inner * outer * s_dev
    height = min(px, 512)
    cols = rest.shape[0]
    return pl.pallas_call(
        functools.partial(direct_kernel, scale=scale),
        grid=(px // height,),
        in_specs=[
            pl.BlockSpec(source.shape, lambda i: (0, 0, 0, 0)),
            pl.BlockSpec((cols, chans), lambda i: (0, 0)),
            pl.BlockSpec((WIDE, WIDE), lambda i: (0, 0)),
            pl.BlockSpec((1, WIDE), lambda i: (0, 0)),
            pl.BlockSpec((WIDE, WIDE), lambda i: (0, 0)),
        ],
        out_specs=pl.BlockSpec((height, cols), lambda i: (i, 0)),
        out_shape=jax.ShapeDtypeStruct((px, cols), jnp.bfloat16),
        compiler_params=PARAMS,
        cost_estimate=cost_of(px, cols, chans),
    )(source, rest, *wide)


def near_kernel(src_ref, tgt_ref, w_ref, b_ref, p_ref, *rest, scale, group):
    outs = rest[-group:]
    inner, _, s_dev, _ = src_ref.shape
    lane = lax.rem(lax.axis_index("src"), inner)
    rows = [src_ref[lane ^ (k % inner), k // inner] for k in partners(group)]

    def store(i, tok):
        for k in range(group):
            outs[k][:, i * WIDE:(i + 1) * WIDE] = tok[k * s_dev:(k + 1) * s_dev, :]

    pipeline_tokens(jnp.concatenate(rows), tgt_ref, w_ref, b_ref, p_ref, scale, store)


def near_tokens(source, target, held, group, wide, scale):
    _, _, s_dev, chans = source.shape
    rows = target.shape[0]
    side = 1 if held else 0
    return pl.pallas_call(
        functools.partial(near_kernel, scale=scale, group=group),
        grid=(1,),
        in_specs=[
            pl.BlockSpec(source.shape, lambda i: (0, 0, 0, 0)),
            pl.BlockSpec((rows, chans), lambda i: (0, 0)),
            pl.BlockSpec((WIDE, WIDE), lambda i: (0, 0)),
            pl.BlockSpec((1, WIDE), lambda i: (0, 0)),
            pl.BlockSpec((WIDE, WIDE), lambda i: (0, 0)),
        ] + [ANY] * len(held),
        out_specs=[pl.BlockSpec((s_dev, rows), lambda i: (0, side))] * group,
        out_shape=[jax.ShapeDtypeStruct((s_dev, 2 * rows), jnp.bfloat16)] * group,
        input_output_aliases={5 + k: k for k in range(len(held))},
        compiler_params=PARAMS,
        cost_estimate=cost_of(group * s_dev, rows, chans),
    )(source, target, *wide, *held)


def place_direct_kernel(direct_ref, out_ref, sems):
    n, _, tail = direct_ref.shape
    stride = out_ref.shape[1] // n
    copies = [
        pltpu.make_async_copy(
            direct_ref.at[i], out_ref.at[:, (i + 1) * stride - tail:(i + 1) * stride], sems.at[i]
        )
        for i in range(n)
    ]
    for copy in copies:
        copy.start()
    for copy in copies:
        copy.wait()


def place_direct(direct, width):
    n, s_dev, tail = direct.shape
    return pl.pallas_call(
        place_direct_kernel,
        in_specs=[ANY],
        out_specs=ANY,
        out_shape=jax.ShapeDtypeStruct((s_dev, width), direct.dtype),
        scratch_shapes=[pltpu.SemaphoreType.DMA((n,))],
        compiler_params=SMALL,
        cost_estimate=pl.CostEstimate(flops=0, bytes_accessed=4 * n * s_dev * tail, transcendentals=0),
    )(direct)


def place_near_kernel(*refs):
    parts, out_ref, sems = refs[:-3], refs[-2], refs[-1]
    group = len(parts)
    first = parts[0].shape[1] // 2
    stride = out_ref.shape[1] // (2 * group)
    me = lax.axis_index("src")
    copies = []
    for k, part in enumerate(parts):
        near = me ^ partners(group)[k]
        for side, frm in ((0, near), (1, near ^ group)):
            at = pl.multiple_of(frm * stride, 128)
            copies.append(pltpu.make_async_copy(
                part.at[:, side * first:(side + 1) * first],
                out_ref.at[:, pl.ds(at, first)],
                sems.at[2 * k + side],
            ))
    for copy in copies:
        copy.start()
    for copy in copies:
        copy.wait()


def place_near(parts, held):
    return pl.pallas_call(
        place_near_kernel,
        in_specs=[ANY] * (1 + len(parts)),
        out_specs=ANY,
        out_shape=jax.ShapeDtypeStruct(held.shape, held.dtype),
        scratch_shapes=[pltpu.SemaphoreType.DMA((2 * len(parts),))],
        input_output_aliases={len(parts): 0},
        compiler_params=SMALL,
        cost_estimate=pl.CostEstimate(flops=0, bytes_accessed=2 * held.size, transcendentals=0),
    )(*parts, held)


def per_device(source_feat, target_feat, conv_weight, conv_bias, proj_weight):
    patches, cells, chans = target_feat.shape
    s_dev = source_feat.shape[0]
    scale = chans ** (-0.5)
    n = lax.axis_size("src")
    group, outer = n // 2, n // INNER
    swapped = patches * SWAP_NUM // SWAP_DEN * cells

    patched = target_feat.reshape(-1, chans)

    def exchange(x, bits):
        return lax.ppermute(x, "src", [(i, i ^ bits) for i in range(n)])

    crossed, rest, *wide = prepare(
        patched, swapped, conv_weight, conv_bias, proj_weight
    )
    got = exchange(crossed, group)
    column = jnp.stack([source_feat] + [exchange(source_feat, k * INNER) for k in range(1, outer)])
    rows = [list(range(i, i + INNER)) for i in range(0, n, INNER)]
    source = lax.all_gather(column, "src", axis=0, axis_index_groups=rows)

    direct = direct_tokens(source, rest, wide, scale).reshape(n, s_dev, -1)
    direct = lax.all_to_all(direct, "src", 0, 0, tiled=True)

    near = near_tokens(source, crossed, [], group, wide, scale)
    near = near_tokens(source, got, near, group, wide, scale)
    parts = [exchange(x, k) if k else x for x, k in zip(near, partners(group))]
    return place_near(parts, place_direct(direct, patched.shape[0] // cells * conv_weight.shape[1] * n))


def solution(mesh):
    in_specs = (P(("pair", "src"), None), P(("pair", "src"), None, None), P(), P(), P())
    out_specs = P(("pair", "src"), None)
    return jax.shard_map(
        per_device, mesh=mesh, in_specs=in_specs, out_specs=out_specs, check_vma=False
    )
```

```python
import functools

import jax
import jax.numpy as jnp
from jax import lax
from jax.experimental import pallas as pl
from jax.experimental.pallas import tpu as pltpu
from jax.sharding import PartitionSpec as P

WIDE = 256
INNER = 4
SWAP_NUM, SWAP_DEN = 3, 8
COVER = 50
PARAMS = pltpu.CompilerParams(vmem_limit_bytes=20 << 20)
SMALL = pltpu.CompilerParams(vmem_limit_bytes=4 << 20)
ANY = pl.BlockSpec(memory_space=pl.ANY)
HBM = pl.BlockSpec(memory_space=pltpu.HBM)
VMEM = pl.BlockSpec(memory_space=pltpu.VMEM)


def pieces(outer):
    return [0, outer // 2] + [k for k in range(1, outer) if k != outer // 2]


def partners(group):
    return [*range(1, INNER), *range(group - 1, INNER - 1, -1), 0]


def gelu(x):
    return x * (lax.erf(x * 0.7071067811865476) * 0.5 + 0.5)


def pipeline_tokens(source, target_ref, w_ref, b_ref, p_ref, scale, store):
    blocks = target_ref.shape[0] // WIDE
    cost, embedded, hidden = {}, {}, {}
    for i in range(blocks + 2):
        if i < blocks:
            product = lax.dot_general(
                source, target_ref[i * WIDE:(i + 1) * WIDE, :], (((1,), (1,)), ((), ())),
                preferred_element_type=jnp.float32,
            )
            cost[i] = (product * scale).astype(jnp.bfloat16)
        if 0 <= i - 1 < blocks:
            embed = jnp.dot(cost.pop(i - 1), w_ref[...], preferred_element_type=jnp.float32)
            embedded[i - 1] = embed + b_ref[...]
            hidden[i - 1] = gelu(embedded[i - 1]).astype(jnp.bfloat16)
        if 0 <= i - 2:
            mixed = jnp.dot(hidden.pop(i - 2), p_ref[...], preferred_element_type=jnp.float32)
            store(i - 2, (embedded.pop(i - 2) + mixed).astype(jnp.bfloat16))


def prepare_kernel(tgt_ref, w_in, b_in, p_in, cross_ref, rest_ref, ww_ref, wb_ref, wp_ref,
                   w_ref, b_ref, p_ref, sems):
    swapped, total = cross_ref.shape[0], tgt_ref.shape[0]
    small = [
        pltpu.make_async_copy(w_in, w_ref, sems.at[0]),
        pltpu.make_async_copy(b_in, b_ref, sems.at[1]),
        pltpu.make_async_copy(p_in, p_ref, sems.at[2]),
    ]
    large = [
        pltpu.make_async_copy(tgt_ref.at[0:swapped, :], cross_ref, sems.at[3]),
        pltpu.make_async_copy(tgt_ref.at[swapped:total, :], rest_ref, sems.at[4]),
    ]
    for copy in small + large:
        copy.start()
    ww_ref[...] = jnp.zeros_like(ww_ref)
    wp_ref[...] = jnp.zeros_like(wp_ref)
    for copy in small:
        copy.wait()
    cells, emb = w_ref.shape
    for i in range(WIDE // cells):
        ww_ref[i * cells:(i + 1) * cells, i * emb:(i + 1) * emb] = w_ref[...]
        wp_ref[i * emb:(i + 1) * emb, i * emb:(i + 1) * emb] = p_ref[...]
        wb_ref[:, i * emb:(i + 1) * emb] = b_ref[...]
    for copy in large:
        copy.wait()


def prepare(patched, swapped, conv_weight, conv_bias, proj_weight):
    rows, chans = patched.shape
    bias = conv_bias[None, :]
    return pl.pallas_call(
        prepare_kernel,
        in_specs=[HBM] * 4,
        out_specs=[VMEM] * 5,
        out_shape=[
            jax.ShapeDtypeStruct((swapped, chans), patched.dtype),
            jax.ShapeDtypeStruct((rows - swapped, chans), patched.dtype),
            jax.ShapeDtypeStruct((WIDE, WIDE), conv_weight.dtype),
            jax.ShapeDtypeStruct((1, WIDE), conv_bias.dtype),
            jax.ShapeDtypeStruct((WIDE, WIDE), proj_weight.dtype),
        ],
        scratch_shapes=[
            pltpu.VMEM(conv_weight.shape, conv_weight.dtype),
            pltpu.VMEM(bias.shape, bias.dtype),
            pltpu.VMEM(proj_weight.shape, proj_weight.dtype),
            pltpu.SemaphoreType.DMA((5,)),
        ],
        compiler_params=SMALL,
    )(*[pltpu.with_memory_space_constraint(x, pltpu.HBM) for x in (patched, conv_weight, bias, proj_weight)])


def cost_of(px, cols, chans):
    return pl.CostEstimate(
        flops=COVER * 2 * px * cols * (chans + 2 * WIDE),
        bytes_accessed=2 * px * cols + 2 * cols * chans,
        transcendentals=px * cols,
    )


def direct_kernel(src_ref, tgt_ref, w_ref, b_ref, p_ref, out_ref, *, scale):
    inner, outer, s_dev, chans = src_ref.shape
    height = out_ref.shape[0] // s_dev
    mine = lax.axis_index("src") // inner
    begin = pl.program_id(0) * (height // inner)
    rows = []
    for r in range(height):
        bits = mine ^ (begin + r // inner)
        at = jnp.where(bits < outer // 2, bits + 1, bits)
        at = jnp.where(bits == outer // 2, 1, jnp.where(bits == 0, 0, at))
        rows.append(src_ref[r % inner, at])

    def store(i, tok):
        out_ref[:, i * WIDE:(i + 1) * WIDE] = tok

    pipeline_tokens(jnp.concatenate(rows), tgt_ref, w_ref, b_ref, p_ref, scale, store)


def direct_tokens(source, rest, wide, scale):
    inner, outer, s_dev, chans = source.shape
    px = inner * outer * s_dev
    height = min(px, 512)
    cols = rest.shape[0]
    return pl.pallas_call(
        functools.partial(direct_kernel, scale=scale),
        grid=(px // height,),
        in_specs=[
            pl.BlockSpec(source.shape, lambda i: (0, 0, 0, 0)),
            pl.BlockSpec((cols, chans), lambda i: (0, 0)),
            pl.BlockSpec((WIDE, WIDE), lambda i: (0, 0)),
            pl.BlockSpec((1, WIDE), lambda i: (0, 0)),
            pl.BlockSpec((WIDE, WIDE), lambda i: (0, 0)),
        ],
        out_specs=pl.BlockSpec((height, cols), lambda i: (i, 0)),
        out_shape=jax.ShapeDtypeStruct((px, cols), jnp.bfloat16),
        compiler_params=PARAMS,
        cost_estimate=cost_of(px, cols, chans),
    )(source, rest, *wide)


def near_kernel(src_ref, tgt_ref, w_ref, b_ref, p_ref, *rest, scale, group):
    outs = rest[-group:]
    inner, outer, s_dev, _ = src_ref.shape
    lane = lax.rem(lax.axis_index("src"), inner)
    rows = [src_ref[lane ^ (k % inner), pieces(outer).index(k // inner)] for k in partners(group)]

    def store(i, tok):
        for k in range(group):
            outs[k][:, i * WIDE:(i + 1) * WIDE] = tok[k * s_dev:(k + 1) * s_dev, :]

    pipeline_tokens(jnp.concatenate(rows), tgt_ref, w_ref, b_ref, p_ref, scale, store)


def near_tokens(source, target, held, group, wide, scale):
    _, _, s_dev, chans = source.shape
    rows = target.shape[0]
    side = 1 if held else 0
    return pl.pallas_call(
        functools.partial(near_kernel, scale=scale, group=group),
        grid=(1,),
        in_specs=[
            pl.BlockSpec(source.shape, lambda i: (0, 0, 0, 0)),
            pl.BlockSpec((rows, chans), lambda i: (0, 0)),
            pl.BlockSpec((WIDE, WIDE), lambda i: (0, 0)),
            pl.BlockSpec((1, WIDE), lambda i: (0, 0)),
            pl.BlockSpec((WIDE, WIDE), lambda i: (0, 0)),
        ] + [ANY] * len(held),
        out_specs=[pl.BlockSpec((s_dev, rows), lambda i: (0, side))] * group,
        out_shape=[jax.ShapeDtypeStruct((s_dev, 2 * rows), jnp.bfloat16)] * group,
        input_output_aliases={5 + k: k for k in range(len(held))},
        compiler_params=PARAMS,
        cost_estimate=cost_of(group * s_dev, rows, chans),
    )(source, target, *wide, *held)


def place_direct_kernel(direct_ref, out_ref, sems):
    n, _, tail = direct_ref.shape
    stride = out_ref.shape[1] // n
    copies = [
        pltpu.make_async_copy(
            direct_ref.at[i], out_ref.at[:, (i + 1) * stride - tail:(i + 1) * stride], sems.at[i]
        )
        for i in range(n)
    ]
    for copy in copies:
        copy.start()
    for copy in copies:
        copy.wait()


def place_direct(direct, width):
    n, s_dev, tail = direct.shape
    return pl.pallas_call(
        place_direct_kernel,
        in_specs=[ANY],
        out_specs=ANY,
        out_shape=jax.ShapeDtypeStruct((s_dev, width), direct.dtype),
        scratch_shapes=[pltpu.SemaphoreType.DMA((n,))],
        compiler_params=SMALL,
        cost_estimate=pl.CostEstimate(flops=0, bytes_accessed=4 * n * s_dev * tail, transcendentals=0),
    )(direct)


def place_near_kernel(*refs):
    parts, out_ref, sems = refs[:-3], refs[-2], refs[-1]
    group = len(parts)
    first = parts[0].shape[1] // 2
    stride = out_ref.shape[1] // (2 * group)
    me = lax.axis_index("src")
    copies = []
    for k, part in enumerate(parts):
        near = me ^ partners(group)[k]
        for side, frm in ((0, near), (1, near ^ (2 * group - INNER))):
            at = pl.multiple_of(frm * stride, 128)
            copies.append(pltpu.make_async_copy(
                part.at[:, side * first:(side + 1) * first],
                out_ref.at[:, pl.ds(at, first)],
                sems.at[2 * k + side],
            ))
    for copy in copies:
        copy.start()
    for copy in copies:
        copy.wait()


def place_near(parts, held):
    return pl.pallas_call(
        place_near_kernel,
        in_specs=[ANY] * (1 + len(parts)),
        out_specs=ANY,
        out_shape=jax.ShapeDtypeStruct(held.shape, held.dtype),
        scratch_shapes=[pltpu.SemaphoreType.DMA((2 * len(parts),))],
        input_output_aliases={len(parts): 0},
        compiler_params=SMALL,
        cost_estimate=pl.CostEstimate(flops=0, bytes_accessed=2 * held.size, transcendentals=0),
    )(*parts, held)


def per_device(source_feat, target_feat, conv_weight, conv_bias, proj_weight):
    patches, cells, chans = target_feat.shape
    s_dev = source_feat.shape[0]
    scale = chans ** (-0.5)
    n = lax.axis_size("src")
    group, outer = n // 2, n // INNER
    swapped = patches * SWAP_NUM // SWAP_DEN * cells

    patched = target_feat.reshape(-1, chans)

    def exchange(x, bits):
        return lax.ppermute(x, "src", [(i, i ^ bits) for i in range(n)])

    crossed, rest, *wide = prepare(
        patched, swapped, conv_weight, conv_bias, proj_weight
    )
    got = exchange(crossed, n - INNER)
    column = jnp.stack([exchange(source_feat, k * INNER) if k else source_feat for k in pieces(outer)])
    rows = [list(range(i, i + INNER)) for i in range(0, n, INNER)]
    source = lax.all_gather(column, "src", axis=0, axis_index_groups=rows)

    direct = direct_tokens(source, rest, wide, scale).reshape(n, s_dev, -1)
    direct = lax.all_to_all(direct, "src", 0, 0, tiled=True)

    near = near_tokens(source, crossed, [], group, wide, scale)
    near = near_tokens(source, got, near, group, wide, scale)
    parts = [exchange(x, k) if k else x for x, k in zip(near, partners(group))]
    return place_near(parts, place_direct(direct, patched.shape[0] // cells * conv_weight.shape[1] * n))


def solution(mesh):
    in_specs = (P(("pair", "src"), None), P(("pair", "src"), None, None), P(), P(), P())
    out_specs = P(("pair", "src"), None)
    return jax.shard_map(
        per_device, mesh=mesh, in_specs=in_specs, out_specs=out_specs, check_vma=False
    )
```

```python
import functools

import jax
import jax.numpy as jnp
from jax import lax
from jax.experimental import pallas as pl
from jax.experimental.pallas import tpu as pltpu
from jax.sharding import PartitionSpec as P

WIDE = 256
INNER = 4
SWAP_NUM, SWAP_DEN = 3, 8
COVER = 50
PARAMS = pltpu.CompilerParams(vmem_limit_bytes=20 << 20)
SMALL = pltpu.CompilerParams(vmem_limit_bytes=4 << 20)
ANY = pl.BlockSpec(memory_space=pl.ANY)
HBM = pl.BlockSpec(memory_space=pltpu.HBM)
VMEM = pl.BlockSpec(memory_space=pltpu.VMEM)


def pieces(outer):
    return [0, outer // 2] + [k for k in range(1, outer) if k != outer // 2]


def partners(group):
    return [*range(1, INNER), *range(group - 1, INNER - 1, -1), 0]


def gelu(x):
    return x * (lax.erf(x * 0.7071067811865476) * 0.5 + 0.5)


def pipeline_tokens(source, target_ref, w_ref, b_ref, p_ref, scale, store):
    blocks = target_ref.shape[0] // WIDE
    cost, embedded, hidden = {}, {}, {}
    for i in range(blocks + 2):
        if i < blocks:
            product = lax.dot_general(
                source, target_ref[i * WIDE:(i + 1) * WIDE, :], (((1,), (1,)), ((), ())),
                preferred_element_type=jnp.float32,
            )
            cost[i] = (product * scale).astype(jnp.bfloat16)
        if 0 <= i - 1 < blocks:
            embed = jnp.dot(cost.pop(i - 1), w_ref[...], preferred_element_type=jnp.float32)
            embedded[i - 1] = embed + b_ref[...]
            hidden[i - 1] = gelu(embedded[i - 1]).astype(jnp.bfloat16)
        if 0 <= i - 2:
            mixed = jnp.dot(hidden.pop(i - 2), p_ref[...], preferred_element_type=jnp.float32)
            store(i - 2, (embedded.pop(i - 2) + mixed).astype(jnp.bfloat16))


def pin(*arrays):
    return [pltpu.with_memory_space_constraint(x, pltpu.HBM) for x in arrays]


def crossing_kernel(tgt_ref, out_ref, sem):
    copy = pltpu.make_async_copy(tgt_ref.at[0:out_ref.shape[0], :], out_ref, sem)
    copy.start()
    copy.wait()


def crossing(patched, rows):
    return pl.pallas_call(
        crossing_kernel,
        in_specs=[HBM],
        out_specs=VMEM,
        out_shape=jax.ShapeDtypeStruct((rows, patched.shape[1]), patched.dtype),
        scratch_shapes=[pltpu.SemaphoreType.DMA],
        compiler_params=SMALL,
    )(*pin(patched))


def prepare_kernel(tgt_ref, w_in, b_in, p_in, rest_ref, ww_ref, wb_ref, wp_ref,
                   w_ref, b_ref, p_ref, sems):
    total = tgt_ref.shape[0]
    large = pltpu.make_async_copy(
        tgt_ref.at[total - rest_ref.shape[0]:total, :], rest_ref, sems.at[3]
    )
    small = [
        pltpu.make_async_copy(w_in, w_ref, sems.at[0]),
        pltpu.make_async_copy(b_in, b_ref, sems.at[1]),
        pltpu.make_async_copy(p_in, p_ref, sems.at[2]),
    ]
    for copy in [*small, large]:
        copy.start()
    ww_ref[...] = jnp.zeros_like(ww_ref)
    wp_ref[...] = jnp.zeros_like(wp_ref)
    for copy in small:
        copy.wait()
    cells, emb = w_ref.shape
    for i in range(WIDE // cells):
        ww_ref[i * cells:(i + 1) * cells, i * emb:(i + 1) * emb] = w_ref[...]
        wp_ref[i * emb:(i + 1) * emb, i * emb:(i + 1) * emb] = p_ref[...]
        wb_ref[:, i * emb:(i + 1) * emb] = b_ref[...]
    large.wait()


def prepare(patched, swapped, conv_weight, conv_bias, proj_weight):
    rows, chans = patched.shape
    bias = conv_bias[None, :]
    return pl.pallas_call(
        prepare_kernel,
        in_specs=[HBM] * 4,
        out_specs=[VMEM] * 4,
        out_shape=[
            jax.ShapeDtypeStruct((rows - swapped, chans), patched.dtype),
            jax.ShapeDtypeStruct((WIDE, WIDE), conv_weight.dtype),
            jax.ShapeDtypeStruct((1, WIDE), conv_bias.dtype),
            jax.ShapeDtypeStruct((WIDE, WIDE), proj_weight.dtype),
        ],
        scratch_shapes=[
            pltpu.VMEM(conv_weight.shape, conv_weight.dtype),
            pltpu.VMEM(bias.shape, bias.dtype),
            pltpu.VMEM(proj_weight.shape, proj_weight.dtype),
            pltpu.SemaphoreType.DMA((4,)),
        ],
        compiler_params=SMALL,
    )(*pin(patched, conv_weight, bias, proj_weight))


def cost_of(px, cols, chans):
    return pl.CostEstimate(
        flops=COVER * 2 * px * cols * (chans + 2 * WIDE),
        bytes_accessed=2 * px * cols + 2 * cols * chans,
        transcendentals=px * cols,
    )


def direct_kernel(src_ref, tgt_ref, w_ref, b_ref, p_ref, out_ref, *, scale):
    inner, outer, s_dev, chans = src_ref.shape
    height = out_ref.shape[0] // s_dev
    mine = lax.axis_index("src") // inner
    begin = pl.program_id(0) * (height // inner)
    rows = []
    for r in range(height):
        bits = mine ^ (begin + r // inner)
        at = jnp.where(bits < outer // 2, bits + 1, bits)
        at = jnp.where(bits == outer // 2, 1, jnp.where(bits == 0, 0, at))
        rows.append(src_ref[r % inner, at])

    def store(i, tok):
        out_ref[:, i * WIDE:(i + 1) * WIDE] = tok

    pipeline_tokens(jnp.concatenate(rows), tgt_ref, w_ref, b_ref, p_ref, scale, store)


def direct_tokens(source, rest, wide, scale):
    inner, outer, s_dev, chans = source.shape
    px = inner * outer * s_dev
    height = min(px, 512)
    cols = rest.shape[0]
    return pl.pallas_call(
        functools.partial(direct_kernel, scale=scale),
        grid=(px // height,),
        in_specs=[
            pl.BlockSpec(source.shape, lambda i: (0, 0, 0, 0)),
            pl.BlockSpec((cols, chans), lambda i: (0, 0)),
            pl.BlockSpec((WIDE, WIDE), lambda i: (0, 0)),
            pl.BlockSpec((1, WIDE), lambda i: (0, 0)),
            pl.BlockSpec((WIDE, WIDE), lambda i: (0, 0)),
        ],
        out_specs=pl.BlockSpec((height, cols), lambda i: (i, 0)),
        out_shape=jax.ShapeDtypeStruct((px, cols), jnp.bfloat16),
        compiler_params=PARAMS,
        cost_estimate=cost_of(px, cols, chans),
    )(source, rest, *wide)


def near_kernel(src_ref, tgt_ref, w_ref, b_ref, p_ref, *rest, scale, group):
    outs = rest[-group:]
    inner, outer, s_dev, _ = src_ref.shape
    lane = lax.rem(lax.axis_index("src"), inner)
    rows = [src_ref[lane ^ (k % inner), pieces(outer).index(k // inner)] for k in partners(group)]

    def store(i, tok):
        for k in range(group):
            outs[k][:, i * WIDE:(i + 1) * WIDE] = tok[k * s_dev:(k + 1) * s_dev, :]

    pipeline_tokens(jnp.concatenate(rows), tgt_ref, w_ref, b_ref, p_ref, scale, store)


def near_tokens(source, target, held, group, wide, scale):
    _, _, s_dev, chans = source.shape
    rows = target.shape[0]
    side = 1 if held else 0
    return pl.pallas_call(
        functools.partial(near_kernel, scale=scale, group=group),
        grid=(1,),
        in_specs=[
            pl.BlockSpec(source.shape, lambda i: (0, 0, 0, 0)),
            pl.BlockSpec((rows, chans), lambda i: (0, 0)),
            pl.BlockSpec((WIDE, WIDE), lambda i: (0, 0)),
            pl.BlockSpec((1, WIDE), lambda i: (0, 0)),
            pl.BlockSpec((WIDE, WIDE), lambda i: (0, 0)),
        ] + [ANY] * len(held),
        out_specs=[pl.BlockSpec((s_dev, rows), lambda i: (0, side))] * group,
        out_shape=[jax.ShapeDtypeStruct((s_dev, 2 * rows), jnp.bfloat16)] * group,
        input_output_aliases={5 + k: k for k in range(len(held))},
        compiler_params=PARAMS,
        cost_estimate=cost_of(group * s_dev, rows, chans),
    )(source, target, *wide, *held)


def place_direct_kernel(direct_ref, out_ref, sems):
    n, _, tail = direct_ref.shape
    stride = out_ref.shape[1] // n
    copies = [
        pltpu.make_async_copy(
            direct_ref.at[i], out_ref.at[:, (i + 1) * stride - tail:(i + 1) * stride], sems.at[i]
        )
        for i in range(n)
    ]
    for copy in copies:
        copy.start()
    for copy in copies:
        copy.wait()


def place_direct(direct, width):
    n, s_dev, tail = direct.shape
    return pl.pallas_call(
        place_direct_kernel,
        in_specs=[ANY],
        out_specs=ANY,
        out_shape=jax.ShapeDtypeStruct((s_dev, width), direct.dtype),
        scratch_shapes=[pltpu.SemaphoreType.DMA((n,))],
        compiler_params=SMALL,
        cost_estimate=pl.CostEstimate(flops=0, bytes_accessed=4 * n * s_dev * tail, transcendentals=0),
    )(direct)


def place_near_kernel(*refs):
    parts, out_ref, sems = refs[:-3], refs[-2], refs[-1]
    group = len(parts)
    first = parts[0].shape[1] // 2
    stride = out_ref.shape[1] // (2 * group)
    me = lax.axis_index("src")
    copies = []
    for k, part in enumerate(parts):
        near = me ^ partners(group)[k]
        for side, frm in ((0, near), (1, near ^ (2 * group - INNER))):
            at = pl.multiple_of(frm * stride, 128)
            copies.append(pltpu.make_async_copy(
                part.at[:, side * first:(side + 1) * first],
                out_ref.at[:, pl.ds(at, first)],
                sems.at[2 * k + side],
            ))
    for copy in copies:
        copy.start()
    for copy in copies:
        copy.wait()


def place_near(parts, held):
    return pl.pallas_call(
        place_near_kernel,
        in_specs=[ANY] * (1 + len(parts)),
        out_specs=ANY,
        out_shape=jax.ShapeDtypeStruct(held.shape, held.dtype),
        scratch_shapes=[pltpu.SemaphoreType.DMA((2 * len(parts),))],
        input_output_aliases={len(parts): 0},
        compiler_params=SMALL,
        cost_estimate=pl.CostEstimate(flops=0, bytes_accessed=2 * held.size, transcendentals=0),
    )(*parts, held)


def per_device(source_feat, target_feat, conv_weight, conv_bias, proj_weight):
    patches, cells, chans = target_feat.shape
    s_dev = source_feat.shape[0]
    scale = chans ** (-0.5)
    n = lax.axis_size("src")
    group, outer = n // 2, n // INNER
    swapped = patches * SWAP_NUM // SWAP_DEN * cells

    patched = target_feat.reshape(-1, chans)

    def exchange(x, bits):
        return lax.ppermute(x, "src", [(i, i ^ bits) for i in range(n)])

    crossed = crossing(patched, swapped)
    rest, *wide = prepare(patched, swapped, conv_weight, conv_bias, proj_weight)
    got = exchange(crossed, n - INNER)
    column = jnp.stack([exchange(source_feat, k * INNER) if k else source_feat for k in pieces(outer)])
    rows = [list(range(i, i + INNER)) for i in range(0, n, INNER)]
    source = lax.all_gather(column, "src", axis=0, axis_index_groups=rows)

    direct = direct_tokens(source, rest, wide, scale).reshape(n, s_dev, -1)
    direct = lax.all_to_all(direct, "src", 0, 0, tiled=True)

    near = near_tokens(source, crossed, [], group, wide, scale)
    near = near_tokens(source, got, near, group, wide, scale)
    parts = [exchange(x, k) if k else x for x, k in zip(near, partners(group))]
    return place_near(parts, place_direct(direct, patched.shape[0] // cells * conv_weight.shape[1] * n))


def solution(mesh):
    in_specs = (P(("pair", "src"), None), P(("pair", "src"), None, None), P(), P(), P())
    out_specs = P(("pair", "src"), None)
    return jax.shard_map(
        per_device, mesh=mesh, in_specs=in_specs, out_specs=out_specs, check_vma=False
    )
```

```python
import functools

import jax
import jax.numpy as jnp
from jax import lax
from jax.experimental import pallas as pl
from jax.experimental.pallas import tpu as pltpu
from jax.sharding import PartitionSpec as P

WIDE = 256
INNER = 4
SWAP_NUM, SWAP_DEN = 3, 8
COVER = 50
PARAMS = pltpu.CompilerParams(vmem_limit_bytes=20 << 20)
SMALL = pltpu.CompilerParams(vmem_limit_bytes=4 << 20)
ANY = pl.BlockSpec(memory_space=pl.ANY)
HBM = pl.BlockSpec(memory_space=pltpu.HBM)
VMEM = pl.BlockSpec(memory_space=pltpu.VMEM)


def pieces(outer):
    return [0, outer // 2] + [k for k in range(1, outer) if k != outer // 2]


def partners(group):
    return [*range(1, INNER), *range(group - 1, INNER - 1, -1), 0]


def gelu(x):
    return x * (lax.erf(x * 0.7071067811865476) * 0.5 + 0.5)


def pipeline_tokens(source, target_ref, w_ref, b_ref, p_ref, scale, store):
    blocks = target_ref.shape[0] // WIDE
    cost, embedded, hidden = {}, {}, {}
    for i in range(blocks + 2):
        if i < blocks:
            product = lax.dot_general(
                source, target_ref[i * WIDE:(i + 1) * WIDE, :], (((1,), (1,)), ((), ())),
                preferred_element_type=jnp.float32,
            )
            cost[i] = (product * scale).astype(jnp.bfloat16)
        if 0 <= i - 1 < blocks:
            embed = jnp.dot(cost.pop(i - 1), w_ref[...], preferred_element_type=jnp.float32)
            embedded[i - 1] = embed + b_ref[...]
            hidden[i - 1] = gelu(embedded[i - 1]).astype(jnp.bfloat16)
        if 0 <= i - 2:
            mixed = jnp.dot(hidden.pop(i - 2), p_ref[...], preferred_element_type=jnp.float32)
            store(i - 2, (embedded.pop(i - 2) + mixed).astype(jnp.bfloat16))


def pin(*arrays):
    return [pltpu.with_memory_space_constraint(x, pltpu.HBM) for x in arrays]


def crossing_kernel(tgt_ref, out_ref, sem):
    copy = pltpu.make_async_copy(tgt_ref.at[0:out_ref.shape[0], :], out_ref, sem)
    copy.start()
    copy.wait()


def crossing(patched, rows):
    return pl.pallas_call(
        crossing_kernel,
        in_specs=[HBM],
        out_specs=VMEM,
        out_shape=jax.ShapeDtypeStruct((rows, patched.shape[1]), patched.dtype),
        scratch_shapes=[pltpu.SemaphoreType.DMA],
        compiler_params=SMALL,
    )(*pin(patched))


def prepare_kernel(tgt_ref, w_in, b_in, p_in, rest_ref, ww_ref, wb_ref, wp_ref,
                   w_ref, b_ref, p_ref, sems):
    total = tgt_ref.shape[0]
    large = pltpu.make_async_copy(
        tgt_ref.at[total - rest_ref.shape[0]:total, :], rest_ref, sems.at[3]
    )
    small = [
        pltpu.make_async_copy(w_in, w_ref, sems.at[0]),
        pltpu.make_async_copy(b_in, b_ref, sems.at[1]),
        pltpu.make_async_copy(p_in, p_ref, sems.at[2]),
    ]
    for copy in [*small, large]:
        copy.start()
    ww_ref[...] = jnp.zeros_like(ww_ref)
    wp_ref[...] = jnp.zeros_like(wp_ref)
    for copy in small:
        copy.wait()
    cells, emb = w_ref.shape
    for i in range(WIDE // cells):
        ww_ref[i * cells:(i + 1) * cells, i * emb:(i + 1) * emb] = w_ref[...]
        wp_ref[i * emb:(i + 1) * emb, i * emb:(i + 1) * emb] = p_ref[...]
        wb_ref[:, i * emb:(i + 1) * emb] = b_ref[...]
    large.wait()


def prepare(patched, swapped, conv_weight, conv_bias, proj_weight):
    rows, chans = patched.shape
    bias = conv_bias[None, :]
    return pl.pallas_call(
        prepare_kernel,
        in_specs=[HBM] * 4,
        out_specs=[VMEM] * 4,
        out_shape=[
            jax.ShapeDtypeStruct((rows - swapped, chans), patched.dtype),
            jax.ShapeDtypeStruct((WIDE, WIDE), conv_weight.dtype),
            jax.ShapeDtypeStruct((1, WIDE), conv_bias.dtype),
            jax.ShapeDtypeStruct((WIDE, WIDE), proj_weight.dtype),
        ],
        scratch_shapes=[
            pltpu.VMEM(conv_weight.shape, conv_weight.dtype),
            pltpu.VMEM(bias.shape, bias.dtype),
            pltpu.VMEM(proj_weight.shape, proj_weight.dtype),
            pltpu.SemaphoreType.DMA((4,)),
        ],
        compiler_params=SMALL,
    )(*pin(patched, conv_weight, bias, proj_weight))


def cost_of(px, cols, chans):
    return pl.CostEstimate(
        flops=COVER * 2 * px * cols * (chans + 2 * WIDE),
        bytes_accessed=2 * px * cols + 2 * cols * chans,
        transcendentals=px * cols,
    )


def direct_kernel(src_ref, tgt_ref, w_ref, b_ref, p_ref, out_ref, *, scale):
    inner, outer, s_dev, chans = src_ref.shape
    height = out_ref.shape[0] // s_dev
    mine = lax.axis_index("src") // inner
    begin = pl.program_id(0) * (height // inner)
    rows = []
    for r in range(height):
        bits = mine ^ (begin + r // inner)
        at = jnp.where(bits < outer // 2, bits + 1, bits)
        at = jnp.where(bits == outer // 2, 1, jnp.where(bits == 0, 0, at))
        rows.append(src_ref[r % inner, at])

    def store(i, tok):
        out_ref[:, i * WIDE:(i + 1) * WIDE] = tok

    pipeline_tokens(jnp.concatenate(rows), tgt_ref, w_ref, b_ref, p_ref, scale, store)


def direct_tokens(source, rest, wide, scale):
    inner, outer, s_dev, chans = source.shape
    px = inner * outer * s_dev
    height = min(px, 512)
    cols = rest.shape[0]
    return pl.pallas_call(
        functools.partial(direct_kernel, scale=scale),
        grid=(px // height,),
        in_specs=[
            pl.BlockSpec(source.shape, lambda i: (0, 0, 0, 0)),
            pl.BlockSpec((cols, chans), lambda i: (0, 0)),
            pl.BlockSpec((WIDE, WIDE), lambda i: (0, 0)),
            pl.BlockSpec((1, WIDE), lambda i: (0, 0)),
            pl.BlockSpec((WIDE, WIDE), lambda i: (0, 0)),
        ],
        out_specs=pl.BlockSpec((height, cols), lambda i: (i, 0)),
        out_shape=jax.ShapeDtypeStruct((px, cols), jnp.bfloat16),
        compiler_params=PARAMS,
        cost_estimate=cost_of(px, cols, chans),
    )(source, rest, *wide)


def near_kernel(src_ref, tgt_ref, w_ref, b_ref, p_ref, *rest, scale, group):
    outs = rest[-group:]
    inner, outer, s_dev, _ = src_ref.shape
    lane = lax.rem(lax.axis_index("src"), inner)
    rows = [src_ref[lane ^ (k % inner), pieces(outer).index(k // inner)] for k in partners(group)]

    def store(i, tok):
        for k in range(group):
            outs[k][:, i * WIDE:(i + 1) * WIDE] = tok[k * s_dev:(k + 1) * s_dev, :]

    pipeline_tokens(jnp.concatenate(rows), tgt_ref, w_ref, b_ref, p_ref, scale, store)


def near_tokens(source, target, held, group, wide, scale):
    _, _, s_dev, chans = source.shape
    rows = target.shape[0]
    side = 1 if held else 0
    return pl.pallas_call(
        functools.partial(near_kernel, scale=scale, group=group),
        grid=(1,),
        in_specs=[
            pl.BlockSpec(source.shape, lambda i: (0, 0, 0, 0)),
            pl.BlockSpec((rows, chans), lambda i: (0, 0)),
            pl.BlockSpec((WIDE, WIDE), lambda i: (0, 0)),
            pl.BlockSpec((1, WIDE), lambda i: (0, 0)),
            pl.BlockSpec((WIDE, WIDE), lambda i: (0, 0)),
        ] + [ANY] * len(held),
        out_specs=[pl.BlockSpec((s_dev, rows), lambda i: (0, side))] * group,
        out_shape=[jax.ShapeDtypeStruct((s_dev, 2 * rows), jnp.bfloat16)] * group,
        input_output_aliases={5 + k: k for k in range(len(held))},
        compiler_params=PARAMS,
        cost_estimate=cost_of(group * s_dev, rows, chans),
    )(source, target, *wide, *held)


def run_all(copies):
    for copy in copies:
        copy.start()
    for copy in copies:
        copy.wait()


def place_direct_kernel(direct_ref, held_ref, out_ref, sems):
    n, _, tail = direct_ref.shape
    stride = out_ref.shape[1] // n
    run_all([
        pltpu.make_async_copy(
            direct_ref.at[i], out_ref.at[:, (i + 1) * stride - tail:(i + 1) * stride], sems.at[i]
        )
        for i in range(n)
    ])


def place_direct(direct, held):
    n, s_dev, tail = direct.shape
    return pl.pallas_call(
        place_direct_kernel,
        in_specs=[ANY] * 2,
        out_specs=ANY,
        out_shape=jax.ShapeDtypeStruct(held.shape, held.dtype),
        scratch_shapes=[pltpu.SemaphoreType.DMA((n,))],
        input_output_aliases={1: 0},
        compiler_params=SMALL,
        cost_estimate=pl.CostEstimate(flops=0, bytes_accessed=4 * n * s_dev * tail, transcendentals=0),
    )(direct, held)


def place_near_kernel(*refs, bits, group):
    parts, out_ref, sems = refs[:len(bits)], refs[-2], refs[-1]
    first = parts[0].shape[1] // 2
    stride = out_ref.shape[1] // (2 * group)
    me = lax.axis_index("src")
    copies = []
    for i, k in enumerate(bits):
        near = me ^ k
        for side, frm in ((0, near), (1, near ^ (2 * group - INNER))):
            at = pl.multiple_of(frm * stride, 128)
            copies.append(pltpu.make_async_copy(
                parts[i].at[:, side * first:(side + 1) * first],
                out_ref.at[:, pl.ds(at, first)],
                sems.at[2 * i + side],
            ))
    run_all(copies)


def place_near(parts, bits, group, shape, held=()):
    return pl.pallas_call(
        functools.partial(place_near_kernel, bits=bits, group=group),
        in_specs=[ANY] * (len(parts) + len(held)),
        out_specs=ANY,
        out_shape=jax.ShapeDtypeStruct(shape, parts[0].dtype),
        scratch_shapes=[pltpu.SemaphoreType.DMA((2 * len(parts),))],
        input_output_aliases={len(parts): 0} if held else {},
        compiler_params=SMALL,
        cost_estimate=pl.CostEstimate(
            flops=0, bytes_accessed=4 * sum(part.size for part in parts), transcendentals=0
        ),
    )(*parts, *held)


def per_device(source_feat, target_feat, conv_weight, conv_bias, proj_weight):
    patches, cells, chans = target_feat.shape
    s_dev = source_feat.shape[0]
    scale = chans ** (-0.5)
    n = lax.axis_size("src")
    group, outer = n // 2, n // INNER
    swapped = patches * SWAP_NUM // SWAP_DEN * cells

    patched = target_feat.reshape(-1, chans)

    def exchange(x, bits):
        return lax.ppermute(x, "src", [(i, i ^ bits) for i in range(n)])

    crossed = crossing(patched, swapped)
    rest, *wide = prepare(patched, swapped, conv_weight, conv_bias, proj_weight)
    got = exchange(crossed, n - INNER)
    column = jnp.stack([exchange(source_feat, k * INNER) if k else source_feat for k in pieces(outer)])
    rows = [list(range(i, i + INNER)) for i in range(0, n, INNER)]
    source = lax.all_gather(column, "src", axis=0, axis_index_groups=rows)

    direct = direct_tokens(source, rest, wide, scale).reshape(n, s_dev, -1)
    direct = lax.all_to_all(direct, "src", 0, 0, tiled=True)

    near = near_tokens(source, crossed, [], group, wide, scale)
    near = near_tokens(source, got, near, group, wide, scale)
    parts = {k: exchange(x, k) if k else x for x, k in zip(near, partners(group))}
    soon = [1, 2, 0]
    late = [k for k in partners(group) if k not in soon]
    shape = (s_dev, n * patches * conv_weight.shape[1])
    out = place_near([parts[k] for k in soon], soon, group, shape)
    out = place_direct(direct, out)
    return place_near([parts[k] for k in late], late, group, shape, [out])


def solution(mesh):
    in_specs = (P(("pair", "src"), None), P(("pair", "src"), None, None), P(), P(), P())
    out_specs = P(("pair", "src"), None)
    return jax.shard_map(
        per_device, mesh=mesh, in_specs=in_specs, out_specs=out_specs, check_vma=False
    )
```

```python
import functools

import jax
import jax.numpy as jnp
from jax import lax
from jax.experimental import pallas as pl
from jax.experimental.pallas import tpu as pltpu
from jax.sharding import PartitionSpec as P

WIDE = 256
INNER = 4
SWAP_NUM, SWAP_DEN = 3, 8
COVER = 50
PARAMS = pltpu.CompilerParams(vmem_limit_bytes=20 << 20)
SMALL = pltpu.CompilerParams(vmem_limit_bytes=4 << 20)
ANY = pl.BlockSpec(memory_space=pl.ANY)
HBM = pl.BlockSpec(memory_space=pltpu.HBM)
VMEM = pl.BlockSpec(memory_space=pltpu.VMEM)


def pieces(outer):
    return [0, outer // 2] + [k for k in range(1, outer) if k != outer // 2]


def partners(group):
    return [1, 2, *range(group - 1, INNER - 1, -1), 3, 0]


def gelu(x):
    return x * (lax.erf(x * 0.7071067811865476) * 0.5 + 0.5)


def pipeline_tokens(source, target_ref, w_ref, b_ref, p_ref, scale, store):
    blocks = target_ref.shape[0] // WIDE
    cost, embedded, hidden = {}, {}, {}
    for i in range(blocks + 2):
        if i < blocks:
            product = lax.dot_general(
                source, target_ref[i * WIDE:(i + 1) * WIDE, :], (((1,), (1,)), ((), ())),
                preferred_element_type=jnp.float32,
            )
            cost[i] = (product * scale).astype(jnp.bfloat16)
        if 0 <= i - 1 < blocks:
            embed = jnp.dot(cost.pop(i - 1), w_ref[...], preferred_element_type=jnp.float32)
            embedded[i - 1] = embed + b_ref[...]
            hidden[i - 1] = gelu(embedded[i - 1]).astype(jnp.bfloat16)
        if 0 <= i - 2:
            mixed = jnp.dot(hidden.pop(i - 2), p_ref[...], preferred_element_type=jnp.float32)
            store(i - 2, (embedded.pop(i - 2) + mixed).astype(jnp.bfloat16))


def pin(*arrays):
    return [pltpu.with_memory_space_constraint(x, pltpu.HBM) for x in arrays]


def crossing_kernel(tgt_ref, out_ref, sem):
    copy = pltpu.make_async_copy(tgt_ref.at[0:out_ref.shape[0], :], out_ref, sem)
    copy.start()
    copy.wait()


def crossing(patched, rows):
    return pl.pallas_call(
        crossing_kernel,
        in_specs=[HBM],
        out_specs=VMEM,
        out_shape=jax.ShapeDtypeStruct((rows, patched.shape[1]), patched.dtype),
        scratch_shapes=[pltpu.SemaphoreType.DMA],
        compiler_params=SMALL,
    )(*pin(patched))


def prepare_kernel(tgt_ref, w_in, b_in, p_in, rest_ref, ww_ref, wb_ref, wp_ref,
                   w_ref, b_ref, p_ref, sems):
    total = tgt_ref.shape[0]
    large = pltpu.make_async_copy(
        tgt_ref.at[total - rest_ref.shape[0]:total, :], rest_ref, sems.at[3]
    )
    small = [
        pltpu.make_async_copy(w_in, w_ref, sems.at[0]),
        pltpu.make_async_copy(b_in, b_ref, sems.at[1]),
        pltpu.make_async_copy(p_in, p_ref, sems.at[2]),
    ]
    for copy in [*small, large]:
        copy.start()
    ww_ref[...] = jnp.zeros_like(ww_ref)
    wp_ref[...] = jnp.zeros_like(wp_ref)
    for copy in small:
        copy.wait()
    cells, emb = w_ref.shape
    for i in range(WIDE // cells):
        ww_ref[i * cells:(i + 1) * cells, i * emb:(i + 1) * emb] = w_ref[...]
        wp_ref[i * emb:(i + 1) * emb, i * emb:(i + 1) * emb] = p_ref[...]
        wb_ref[:, i * emb:(i + 1) * emb] = b_ref[...]
    large.wait()


def prepare(patched, swapped, conv_weight, conv_bias, proj_weight):
    rows, chans = patched.shape
    bias = conv_bias[None, :]
    return pl.pallas_call(
        prepare_kernel,
        in_specs=[HBM] * 4,
        out_specs=[VMEM] * 4,
        out_shape=[
            jax.ShapeDtypeStruct((rows - swapped, chans), patched.dtype),
            jax.ShapeDtypeStruct((WIDE, WIDE), conv_weight.dtype),
            jax.ShapeDtypeStruct((1, WIDE), conv_bias.dtype),
            jax.ShapeDtypeStruct((WIDE, WIDE), proj_weight.dtype),
        ],
        scratch_shapes=[
            pltpu.VMEM(conv_weight.shape, conv_weight.dtype),
            pltpu.VMEM(bias.shape, bias.dtype),
            pltpu.VMEM(proj_weight.shape, proj_weight.dtype),
            pltpu.SemaphoreType.DMA((4,)),
        ],
        compiler_params=SMALL,
    )(*pin(patched, conv_weight, bias, proj_weight))


def cost_of(px, cols, chans):
    return pl.CostEstimate(
        flops=COVER * 2 * px * cols * (chans + 2 * WIDE),
        bytes_accessed=2 * px * cols + 2 * cols * chans,
        transcendentals=px * cols,
    )


def direct_kernel(src_ref, tgt_ref, w_ref, b_ref, p_ref, out_ref, *, scale):
    inner, outer, s_dev, chans = src_ref.shape
    height = out_ref.shape[0] // s_dev
    mine = lax.axis_index("src") // inner
    begin = pl.program_id(0) * (height // inner)
    rows = []
    for r in range(height):
        bits = mine ^ (begin + r // inner)
        at = jnp.where(bits < outer // 2, bits + 1, bits)
        at = jnp.where(bits == outer // 2, 1, jnp.where(bits == 0, 0, at))
        rows.append(src_ref[r % inner, at])

    def store(i, tok):
        out_ref[:, i * WIDE:(i + 1) * WIDE] = tok

    pipeline_tokens(jnp.concatenate(rows), tgt_ref, w_ref, b_ref, p_ref, scale, store)


def direct_tokens(source, rest, wide, scale):
    inner, outer, s_dev, chans = source.shape
    px = inner * outer * s_dev
    height = min(px, 512)
    cols = rest.shape[0]
    return pl.pallas_call(
        functools.partial(direct_kernel, scale=scale),
        grid=(px // height,),
        in_specs=[
            pl.BlockSpec(source.shape, lambda i: (0, 0, 0, 0)),
            pl.BlockSpec((cols, chans), lambda i: (0, 0)),
            pl.BlockSpec((WIDE, WIDE), lambda i: (0, 0)),
            pl.BlockSpec((1, WIDE), lambda i: (0, 0)),
            pl.BlockSpec((WIDE, WIDE), lambda i: (0, 0)),
        ],
        out_specs=pl.BlockSpec((height, cols), lambda i: (i, 0)),
        out_shape=jax.ShapeDtypeStruct((px, cols), jnp.bfloat16),
        compiler_params=PARAMS,
        cost_estimate=cost_of(px, cols, chans),
    )(source, rest, *wide)


def near_kernel(src_ref, tgt_ref, w_ref, b_ref, p_ref, *rest, scale, group):
    outs = rest[-group:]
    inner, outer, s_dev, _ = src_ref.shape
    lane = lax.rem(lax.axis_index("src"), inner)
    rows = [src_ref[lane ^ (k % inner), pieces(outer).index(k // inner)] for k in partners(group)]

    def store(i, tok):
        for k in range(group):
            outs[k][:, i * WIDE:(i + 1) * WIDE] = tok[k * s_dev:(k + 1) * s_dev, :]

    pipeline_tokens(jnp.concatenate(rows), tgt_ref, w_ref, b_ref, p_ref, scale, store)


def near_tokens(source, target, held, group, wide, scale):
    _, _, s_dev, chans = source.shape
    rows = target.shape[0]
    side = 1 if held else 0
    return pl.pallas_call(
        functools.partial(near_kernel, scale=scale, group=group),
        grid=(1,),
        in_specs=[
            pl.BlockSpec(source.shape, lambda i: (0, 0, 0, 0)),
            pl.BlockSpec((rows, chans), lambda i: (0, 0)),
            pl.BlockSpec((WIDE, WIDE), lambda i: (0, 0)),
            pl.BlockSpec((1, WIDE), lambda i: (0, 0)),
            pl.BlockSpec((WIDE, WIDE), lambda i: (0, 0)),
        ] + [ANY] * len(held),
        out_specs=[pl.BlockSpec((s_dev, rows), lambda i: (0, side))] * group,
        out_shape=[jax.ShapeDtypeStruct((s_dev, 2 * rows), jnp.bfloat16)] * group,
        input_output_aliases={5 + k: k for k in range(len(held))},
        compiler_params=PARAMS,
        cost_estimate=cost_of(group * s_dev, rows, chans),
    )(source, target, *wide, *held)


def run_all(copies):
    for copy in copies:
        copy.start()
    for copy in copies:
        copy.wait()


def place_direct_kernel(direct_ref, held_ref, out_ref, sems):
    n, _, tail = direct_ref.shape
    stride = out_ref.shape[1] // n
    run_all([
        pltpu.make_async_copy(
            direct_ref.at[i], out_ref.at[:, (i + 1) * stride - tail:(i + 1) * stride], sems.at[i]
        )
        for i in range(n)
    ])


def place_direct(direct, held):
    n, s_dev, tail = direct.shape
    return pl.pallas_call(
        place_direct_kernel,
        in_specs=[ANY] * 2,
        out_specs=ANY,
        out_shape=jax.ShapeDtypeStruct(held.shape, held.dtype),
        scratch_shapes=[pltpu.SemaphoreType.DMA((n,))],
        input_output_aliases={1: 0},
        compiler_params=SMALL,
        cost_estimate=pl.CostEstimate(flops=0, bytes_accessed=4 * n * s_dev * tail, transcendentals=0),
    )(direct, held)


def place_near_kernel(*refs, bits, group):
    parts, out_ref, sems = refs[:len(bits)], refs[-2], refs[-1]
    first = parts[0].shape[1] // 2
    stride = out_ref.shape[1] // (2 * group)
    me = lax.axis_index("src")
    copies = []
    for i, k in enumerate(bits):
        near = me ^ k
        for side, frm in ((0, near), (1, near ^ (2 * group - INNER))):
            at = pl.multiple_of(frm * stride, 128)
            copies.append(pltpu.make_async_copy(
                parts[i].at[:, side * first:(side + 1) * first],
                out_ref.at[:, pl.ds(at, first)],
                sems.at[2 * i + side],
            ))
    run_all(copies)


def place_near(parts, bits, group, shape, held=()):
    return pl.pallas_call(
        functools.partial(place_near_kernel, bits=bits, group=group),
        in_specs=[ANY] * (len(parts) + len(held)),
        out_specs=ANY,
        out_shape=jax.ShapeDtypeStruct(shape, parts[0].dtype),
        scratch_shapes=[pltpu.SemaphoreType.DMA((2 * len(parts),))],
        input_output_aliases={len(parts): 0} if held else {},
        compiler_params=SMALL,
        cost_estimate=pl.CostEstimate(
            flops=0, bytes_accessed=4 * sum(part.size for part in parts), transcendentals=0
        ),
    )(*parts, *held)


def per_device(source_feat, target_feat, conv_weight, conv_bias, proj_weight):
    patches, cells, chans = target_feat.shape
    s_dev = source_feat.shape[0]
    scale = chans ** (-0.5)
    n = lax.axis_size("src")
    group, outer = n // 2, n // INNER
    swapped = patches * SWAP_NUM // SWAP_DEN * cells

    patched = target_feat.reshape(-1, chans)

    def exchange(x, bits):
        return lax.ppermute(x, "src", [(i, i ^ bits) for i in range(n)])

    crossed = crossing(patched, swapped)
    rest, *wide = prepare(patched, swapped, conv_weight, conv_bias, proj_weight)
    got = exchange(crossed, n - INNER)
    column = jnp.stack([exchange(source_feat, k * INNER) if k else source_feat for k in pieces(outer)])
    rows = [list(range(i, i + INNER)) for i in range(0, n, INNER)]
    source = lax.all_gather(column, "src", axis=0, axis_index_groups=rows)

    direct = direct_tokens(source, rest, wide, scale).reshape(n, s_dev, -1)
    direct = lax.all_to_all(direct, "src", 0, 0, tiled=True)

    near = near_tokens(source, crossed, [], group, wide, scale)
    near = near_tokens(source, got, near, group, wide, scale)
    parts = {k: exchange(x, k) if k else x for x, k in zip(near, partners(group))}
    soon = [1, 2, 0]
    late = [k for k in partners(group) if k not in soon]
    shape = (s_dev, n * patches * conv_weight.shape[1])
    out = place_near([parts[k] for k in soon], soon, group, shape)
    out = place_direct(direct, out)
    return place_near([parts[k] for k in late], late, group, shape, [out])


def solution(mesh):
    in_specs = (P(("pair", "src"), None), P(("pair", "src"), None, None), P(), P(), P())
    out_specs = P(("pair", "src"), None)
    return jax.shard_map(
        per_device, mesh=mesh, in_specs=in_specs, out_specs=out_specs, check_vma=False
    )
```
